128 devices in a mesh: rows: 32 (over x, z, core), ch: 4 (over y).
Axes of the slice: x: 4, y: 4, z: 4, core: 2. Of those that a mesh axis runs over, the one named last changes fastest.
Arguments:
- latent: float32 [4, 64, 160, 512], P(None, 'rows', None, 'ch'), may hold values from -12 to 12
- first_weight: float32 [27, 512, 512], P(None, 'ch'), may hold values from -0.0546875 to 0.0546875
- norm_gain: float32 [512], P('ch'), may hold values from 0.5 to 1.5
- norm_shift: float32 [512], P('ch'), may hold values from -3 to 3
- second_weight: float32 [27, 512, 256], replicated, may hold values from -0.0546875 to 0.0546875
- out_bias: float32 [256], replicated, may hold values from -3 to 3
Outputs:
- decoded: float32 [4, 128, 320, 256], P(None, ('rows', 'ch'))
The draws below stay inside these ranges and needn't reach their ends.
All inputs are finite; a program needn't handle non-finite values.
Results may differ from the reference program's by a relative error of at most 0.0001.
Values sent between devices are 32-bit elements; how exact they have to be, the bound alone decides.
No kernel may reach another device: no remote copies, remote signals or barrier semaphores. Data moves between devices by JAX's collectives and lax.ppermute only.
A program may use at most 320 MiB of HBM per device.

```python
import math
import jax
import jax.numpy as jnp
from jax import lax

C1 = 512
C2 = 256
GROUPS = 32
FRAMES = 4
COLS = 160
ROWS_ALL = 64


def draw_latent(key, part):
    keys = jax.random.split(jax.random.fold_in(key, 11), 3)
    positions = jnp.arange(ROWS_ALL, dtype=jnp.float32)
    row_scale = jnp.exp(math.log(3.0) * positions / max(ROWS_ALL - 1, 1)) * jax.random.uniform(keys[0], (ROWS_ALL,), jnp.float32, 0.7, 1.4)
    chan_scale = jnp.exp(jax.random.uniform(keys[1], (C1,), jnp.float32, math.log(0.3), math.log(3.0)))
    shape = (FRAMES, ROWS_ALL, COLS, C1)
    base = jax.random.normal(keys[2], shape, jnp.float32)
    values = base * row_scale[None, :, None, None] * chan_scale
    return jnp.clip(values, -12.0, 12.0)


def shard_levels(stream_key, dims, pieces, smallest, top_value):
    loudness = 1.0
    for dim, shards_of in pieces:
        draws = jax.random.uniform(jax.random.fold_in(jax.random.fold_in(stream_key, 6), dim), (shards_of,), jnp.float32, smallest / len(pieces), top_value / len(pieces))
        loudness = loudness * jnp.repeat(jnp.exp(draws), dims[dim] // shards_of).reshape((-1,) + (1,) * (len(dims) - 1 - dim))
    return loudness


def normal_values(key, extent, deviation, most, cuts=(), held_as=jnp.bfloat16):
    drawn = jax.random.normal(key, extent, jnp.float32) * deviation
    if len(cuts) > 0:
        drawn = shard_levels(key, extent, cuts, -0.22, 0.18) * drawn
    return jnp.clip(drawn, min=-most, max=most).astype(held_as)


def setup_inputs(seed: int = 0) -> dict:
    splits = jax.random.split(jax.random.key(seed), 7)
    latent = draw_latent(jax.random.fold_in(splits[6], 71), 0)
    first_weight = normal_values(splits[1], (27, C1, C1), (27 * C1) ** -0.5, 0.0546875, ((1, 4),), jnp.float32)
    norm_gain = jnp.clip(1.0 + 0.1 * jax.random.normal(splits[2], (C1,), jnp.float32), 0.5, 1.5)
    norm_shift = normal_values(splits[3], (C1,), 0.5, 3.0, ((0, 4),), jnp.float32)
    second_weight = normal_values(splits[4], (27, C1, C2), (27 * C1) ** -0.5, 0.0546875, (), jnp.float32)
    out_bias = normal_values(splits[5], (C2,), 0.5, 3.0, (), jnp.float32)
    return {"latent": latent, "first_weight": first_weight, "norm_gain": norm_gain, "norm_shift": norm_shift, "second_weight": second_weight, "out_bias": out_bias}


epsilon = 1e-06

def pad_edges(field):
    first_frame = field[:1]
    field = jnp.concatenate([first_frame, first_frame, field], axis=0)
    return jnp.pad(field, ((0, 0), (0, 0), (1, 1), (0, 0)))

def convolve(padded, weights, frames, height, breadth):
    inner = padded.shape[-1]
    total = jnp.zeros((frames * height * breadth, weights.shape[-1]), jnp.float32)
    for time_tap in range(3):
        for row_tap in range(3):
            for col_tap in range(3):
                piece = padded[time_tap:time_tap + frames, row_tap:row_tap + height, col_tap:col_tap + breadth, :]
                total = total + jnp.dot(piece.reshape(-1, inner), weights[9 * time_tap + 3 * row_tap + col_tap], precision=lax.Precision.HIGHEST, preferred_element_type=jnp.float32)
    return total.reshape(frames, height, breadth, -1)

def causal_conv(field, weights):
    frames, height, breadth, inner = field.shape
    rimmed = jnp.pad(field, ((0, 0), (1, 1), (0, 0), (0, 0)))
    return convolve(pad_edges(rimmed), weights, frames, height, breadth)

def reference(latent, first_weight, norm_gain, norm_shift, second_weight, out_bias):
    frames, height, breadth, width = latent.shape
    first = causal_conv(latent, first_weight)
    grouped = first.reshape(frames, height, breadth, GROUPS, width // GROUPS)
    mean = lax.optimization_barrier(jnp.mean(grouped, axis=(0, 1, 2, 4), keepdims=True))
    centered = grouped - mean
    variance = lax.optimization_barrier(jnp.mean(centered * centered, axis=(0, 1, 2, 4), keepdims=True))
    normed = (centered / jnp.sqrt(variance + epsilon)).reshape(frames, height, breadth, width)
    hidden = jax.nn.silu(normed * norm_gain + norm_shift)
    upsampled = jnp.repeat(jnp.repeat(hidden, 2, axis=1), 2, axis=2)
    return causal_conv(upsampled, second_weight) + out_bias
```

```python
import functools
import jax
import jax.numpy as jnp
from jax import lax
from jax.experimental import pallas as pl
from jax.experimental.pallas import tpu as pltpu
from jax.sharding import PartitionSpec as P


EPS = 1e-6
F32 = jnp.float32
BF16 = jnp.bfloat16
T, Q, CB, GW = 4, 160, 128, 16
NR, NC = 32, 4
MAT = (0, 0, 1, 1, 2, 3)
VMEM = 60 * 1024 * 1024


def split(v):
    hi = v.astype(BF16)
    return hi, (v - hi.astype(F32)).astype(BF16)


def time_inputs(x0, x1, x2, x3):
    return (x0, (x1 + x2) * 0.5, x1 - x0, x1 - x3, x0 - x2, x2 - x1)


def time_weights(a, b, c):
    ac = a + c
    return (ac + b, c, a, (ac - b) * 0.5)


def time_outputs(s0, s1, c0, c1, a, d):
    return (s0, s0 + c0, a + s1 + d, s1 - d - c1)


def shifted(v, by):
    rows = v.shape[0]
    rolled = pltpu.roll(v, by % rows, axis=0)
    q = lax.broadcasted_iota(jnp.int32, v.shape, 0)
    return jnp.where(q == (0 if by > 0 else rows - 1), 0.0, rolled)


def fill_x(lat, top, bot, x):
    def one(row, get):
        for f, v in enumerate(time_inputs(*(get(t) for t in range(T)))):
            for j in range(3):
                hi, lo = split(v if j == 1 else shifted(v, 1 - j))
                x[f, row, :, j * 256 : j * 256 + 128] = hi
                x[f, row, :, j * 256 + 128 : j * 256 + 256] = lo

    def local(k, carry):
        one(k + 1, lambda t: lat[t, k])
        return carry

    one(0, lambda t: top[t, 0])
    lax.fori_loop(0, 2, local, 0)
    one(3, lambda t: bot[t, 0])


def fill_b(w, b):
    def step(k, carry):
        i, j = k // 3, k % 3
        for m, v in enumerate(time_weights(w[k], w[9 + k], w[18 + k])):
            hi, lo = split(v)
            for half in range(2):
                at = pl.ds(pl.multiple_of(j * 256 + half * 128, 128), 128)
                b[m, i, at, 0:128] = hi
                b[m, i, at, 128:256] = lo
        return carry

    lax.fori_loop(0, 9, step, 0)


def products(x, b, p):
    def step(f, carry):
        m = jnp.where(f < 4, f // 2, f - 2)
        total = None
        for i in range(3):
            lhs = x[f, pl.ds(i, 2)].reshape(2 * Q, 768)
            term = jnp.dot(lhs, b[m, i], preferred_element_type=F32)
            total = term if total is None else total + term
        p[f] = total[:, :128] + total[:, 128:]
        return carry

    lax.fori_loop(0, 6, step, 0)


def store_chunk(p, lo, hi):
    y = time_outputs(*(p[f] for f in range(6)))
    for t in range(T):
        ref = lo if t < 2 else hi
        ref[t % 2] = y[t].reshape(2, Q, CB)


def conv1_first(ids, lat, top, bot, w, lo, hi, x, b, p):
    fill_x(lat, top, bot, x)
    fill_b(w, b)
    products(x, b, p)
    store_chunk(p, lo, hi)


def conv1_more(ids, x, w, lo, hi, b, p):
    fill_b(w, b)
    products(x, b, p)
    store_chunk(p, lo.at[0], hi.at[0])


HALF = jax.ShapeDtypeStruct((2, 2, Q, CB), F32)
XS = (6, 4, Q, 768)
WBLOCK = pl.BlockSpec((27, CB, CB), lambda k, ids: (0, 0, ids[k]))
CONV1_SCRATCH = [pltpu.VMEM((4, 3, 768, 256), BF16), pltpu.VMEM((6, 2 * Q, CB), F32)]


def whole(shape):
    return pl.BlockSpec(shape, lambda k, *ids: (0,) * len(shape))


def run_conv1_first(ids, lat, top, bot, w):
    return pl.pallas_call(
        conv1_first,
        grid_spec=pltpu.PrefetchScalarGridSpec(
            num_scalar_prefetch=1,
            grid=(1,),
            in_specs=[whole(lat.shape), whole(top.shape), whole(bot.shape), WBLOCK],
            out_specs=[whole(HALF.shape), whole(HALF.shape), whole(XS)],
            scratch_shapes=CONV1_SCRATCH,
        ),
        out_shape=[HALF, HALF, jax.ShapeDtypeStruct(XS, BF16)],
        compiler_params=pltpu.CompilerParams(vmem_limit_bytes=VMEM),
        cost_estimate=pl.CostEstimate(flops=4_500_000_000, bytes_accessed=9_000_000, transcendentals=0),
        name="conv1_first",
    )(ids, lat, top, bot, w)


def run_conv1_more(ids, x, w):
    n = ids.shape[0]
    out = pl.BlockSpec((1,) + HALF.shape, lambda k, ids: (k, 0, 0, 0, 0))
    shape = jax.ShapeDtypeStruct((n,) + HALF.shape, F32)
    return pl.pallas_call(
        conv1_more,
        grid_spec=pltpu.PrefetchScalarGridSpec(
            num_scalar_prefetch=1,
            grid=(n,),
            in_specs=[whole(XS), WBLOCK],
            out_specs=[out, out],
            scratch_shapes=CONV1_SCRATCH,
        ),
        out_shape=[shape, shape],
        compiler_params=pltpu.CompilerParams(vmem_limit_bytes=VMEM),
        cost_estimate=pl.CostEstimate(flops=4_500_000_000 * n, bytes_accessed=6_000_000 + 2_000_000 * n, transcendentals=0),
        name="conv1_more",
    )(ids, x, w)


def group_sum(v):
    same = (
        lax.broadcasted_iota(jnp.int32, (CB, CB), 0) // GW
        == lax.broadcasted_iota(jnp.int32, (CB, CB), 1) // GW
    ).astype(F32)
    wide = jnp.broadcast_to(v, (8, CB))
    return jnp.dot(wide, same, precision=lax.Precision.HIGHEST, preferred_element_type=F32)[:1]


def finish_first(own_lo, own_hi, a1, a2, b1, b2, gain, shift, even, odd, stats):
    total = jnp.zeros((8, CB), F32)
    for t in range(T):
        own, u, v = (own_lo, a1, a2) if t < 2 else (own_hi, b1, b2)
        for k, out in enumerate((even, odd)):
            y = own[t % 2, k] + u[t % 2, k] + v[t % 2, k]
            out[t] = y
            total = total + y.reshape(Q // 8, 8, CB).sum(0)
    count = float(T * 2 * Q * GW)
    mean = group_sum(total.sum(0, keepdims=True)) / count
    square = jnp.zeros((8, CB), F32)
    for t in range(T):
        for out in (even, odd):
            d = out[t] - mean
            square = square + (d * d).reshape(Q // 8, 8, CB).sum(0)
    m2 = group_sum(square.sum(0, keepdims=True))
    row = jnp.concatenate([mean, m2, gain[...], shift[...]], axis=0)
    stats[...] = jnp.broadcast_to(row[None], stats.shape)


def run_finish(own_lo, own_hi, a1, a2, b1, b2, gain, shift):
    plane = jax.ShapeDtypeStruct((T, Q, CB), F32)
    return pl.pallas_call(
        finish_first,
        out_shape=[plane, plane, jax.ShapeDtypeStruct((NR * NC, 4, CB), F32)],
        compiler_params=pltpu.CompilerParams(vmem_limit_bytes=VMEM),
        cost_estimate=pl.CostEstimate(flops=2_000_000, bytes_accessed=3_000_000, transcendentals=0),
        name="finish_first",
    )(own_lo, own_hi, a1, a2, b1, b2, gain, shift)


def prep_second(ids, coef, w, out):
    def step(k, carry):
        rows = pl.ds(pl.multiple_of(k * 16, 16), 16)
        for side in range(2):
            c0, c1, c2 = (coef[side * 3 + i] for i in range(3))
            taps = []
            for t in range(3):
                merged = []
                for j in range(3):
                    g = [w[9 * t + 3 * i + j, rows, :] for i in range(3)]
                    merged.append(g[0] * c0 + g[1] * c1 + g[2] * c2)
                taps.append((merged[0] + merged[1] + merged[2], merged[0], merged[2]))
            dst = pl.ds(pl.multiple_of(side * 128 + k * 16, 16), 16)
            for v in range(3):
                for m, value in enumerate(time_weights(taps[0][v], taps[1][v], taps[2][v])):
                    hi, lo = split(value)
                    out[0, m, v, 0, dst, :] = hi
                    out[0, m, v, 1, dst, :] = lo
        return carry

    lax.fori_loop(0, 8, step, 0)


W2S = (4, 4, 3, 2, 256, 256)


def run_prep(ids, coef, w):
    return pl.pallas_call(
        prep_second,
        grid_spec=pltpu.PrefetchScalarGridSpec(
            num_scalar_prefetch=2,
            grid=(4,),
            in_specs=[pl.BlockSpec((27, CB, 256), lambda k, ids, coef: (0, ids[k], 0))],
            out_specs=pl.BlockSpec((1,) + W2S[1:], lambda k, ids, coef: (k, 0, 0, 0, 0, 0)),
        ),
        out_shape=jax.ShapeDtypeStruct(W2S, BF16),
        compiler_params=pltpu.CompilerParams(vmem_limit_bytes=VMEM),
        cost_estimate=pl.CostEstimate(flops=30_000_000, bytes_accessed=27_000_000, transcendentals=0),
        name="prep_second",
    )(ids, coef, w)


def conv2(ids, valid, e0, o0, e1, o1, e2, o2, e3, o3, stats, w, bias, out, raw, h, a, acc, fine):
    s = pl.program_id(0)
    for k, pair in enumerate(((e0, o0), (e1, o1), (e2, o2), (e3, o3))):

        @pl.when(s == k)
        def _():
            for side in range(2):
                raw[side] = pair[side][...]

    block = ids[s]
    count = float(T * 2 * Q * GW)
    means = stats[:, block, 0, :]
    mean = means.sum(0, keepdims=True) / NR
    off = means - mean
    m2 = stats[:, block, 1, :].sum(0, keepdims=True) + count * (off * off).sum(0, keepdims=True)
    scale = stats[0, block, 2:3, :] / jnp.sqrt(m2 / (count * NR) + EPS)
    shift = stats[0, block, 3:4, :]

    def norm(t, carry):
        for side in range(2):
            v = (raw[side, t] - mean) * scale + shift
            v = v / (1.0 + jnp.exp(-v))
            h[t, :, side * 128 : side * 128 + 128] = v * valid[side]
        return carry

    lax.fori_loop(0, T, norm, 0)

    def fill(side, carry):
        lanes = pl.ds(pl.multiple_of(side * 128, 128), 128)
        x = time_inputs(*(h[t, :, lanes] for t in range(T)))
        for f in range(6):
            for v, value in enumerate((x[f], shifted(x[f], 1) - x[f], shifted(x[f], -1) - x[f])):
                hi, lo = split(value)
                a[v, 0, f, :, lanes] = hi
                a[v, 1, f, :, lanes] = lo
        return carry

    lax.fori_loop(0, 2, fill, 0)

    @pl.when(s == 0)
    def _():
        acc[...] = jnp.zeros_like(acc)

    def multiply(v, carry):
        for m, at, n in ((0, 0, 2), (1, 2, 2), (2, 4, 1), (3, 5, 1)):
            both = a[v, :, at : at + n].reshape(2 * n * Q, 256)
            high = jnp.dot(both, w[0, m, v, 0], preferred_element_type=F32)
            low = jnp.dot(
                a[v, 0, at : at + n].reshape(n * Q, 256), w[0, m, v, 1], preferred_element_type=F32
            )
            acc[v, at : at + n] += (high[: n * Q] + high[n * Q :] + low).reshape(n, Q, 256)
        return carry

    lax.fori_loop(0, 3, multiply, 0)

    @pl.when(s == 3)
    def _():
        for half in range(2):
            lanes = slice(half * 128, half * 128 + 128)
            y = time_outputs(*(acc[0, f, :, lanes] for f in range(6)))
            for v in (1, 2):
                z = time_outputs(*(acc[v, f, :, lanes] for f in range(6)))
                for t in range(T):
                    fine[t, pl.ds(v - 1, Q, stride=2), :] = y[t] + z[t] + bias[:, lanes]
            out[:, :, lanes] = fine[...]


def run_conv2(ids, valid, rows, stats, w, bias):
    plane = pl.BlockSpec((T, Q, CB), lambda k, *_: (0, 0, 0))
    return pl.pallas_call(
        conv2,
        grid_spec=pltpu.PrefetchScalarGridSpec(
            num_scalar_prefetch=2,
            grid=(4,),
            in_specs=[plane] * 8
            + [
                whole((NR, NC, 4, CB)),
                pl.BlockSpec((1,) + W2S[1:], lambda k, *_: (k, 0, 0, 0, 0, 0)),
                whole((1, 256)),
            ],
            out_specs=whole((T, 2 * Q, 256)),
            scratch_shapes=[
                pltpu.VMEM((2, T, Q, CB), F32),
                pltpu.VMEM((T, Q, 256), F32),
                pltpu.VMEM((3, 2, 6, Q, 256), BF16),
                pltpu.VMEM((3, 6, Q, 256), F32),
                pltpu.VMEM((T, 2 * Q, 128), F32),
            ],
        ),
        out_shape=jax.ShapeDtypeStruct((T, 2 * Q, 256), F32),
        compiler_params=pltpu.CompilerParams(vmem_limit_bytes=VMEM),
        cost_estimate=pl.CostEstimate(flops=9_000_000_000, bytes_accessed=18_000_000, transcendentals=700_000),
        name="conv2",
    )(ids, valid, *rows, stats, w, bias)


def index(r, c):
    return r * NC + c


def gather_perm(shift, odd):
    pairs = []
    for r in range(NR):
        for p in range(NC):
            q = (p + shift) % NC
            to = r
            if odd and q == 0:
                to = r + 1
            if not odd and q == 3:
                to = r - 1
            if 0 <= to < NR:
                pairs.append((index(r, p), index(to, q)))
    return pairs


def shards(latent, first_weight, norm_gain, norm_shift, second_weight, out_bias):
    c = lax.axis_index("ch")
    r = lax.axis_index("rows")
    both = ("rows", "ch")
    top = lax.ppermute(latent[:, 1:2], "rows", [(i, i + 1) for i in range(NR - 1)])
    bot = lax.ppermute(latent[:, 0:1], "rows", [(i + 1, i) for i in range(NR - 1)])

    def ids(*shifts):
        return jnp.stack([(c + s) % NC for s in shifts]).astype(jnp.int32)

    up = [(i, (i + 1) % NC) for i in range(NC)]
    down = [((i + 1) % NC, i) for i in range(NC)]

    def send(v, perm):
        return lax.ppermute(v, "ch", perm)

    far_lo, far_hi, x = run_conv1_first(ids(2), latent, top, bot, first_weight)
    got_lo, got_hi = send(far_lo, up), send(far_hi, down)
    near_lo, near_hi = run_conv1_more(ids(1, 3), x, first_weight)
    b1, a1 = send(near_hi[0], up), send(near_lo[1], down)
    a2, b2 = send(near_lo[0] + got_lo, up), send(near_hi[1] + got_hi, down)
    own_lo, own_hi = run_conv1_more(ids(0), x, first_weight)
    even, odd, stats = run_finish(
        own_lo[0], own_hi[0], a1, a2, b1, b2, norm_gain[None], norm_shift[None]
    )

    moved = {}
    for s in (1, 3, 2):
        moved[s] = (
            lax.ppermute(even, both, gather_perm(s, False)),
            lax.ppermute(odd, both, gather_perm(s, True)),
        )
    edge = [(index(i, 0), index(i + 1, 0)) for i in range(NR - 1)]
    edge += [(index(i + 1, 3), index(i, 3)) for i in range(NR - 1)]
    halo = lax.ppermute(jnp.where(c == 0, odd, even), both, edge)
    rows = [jnp.where(c == 3, halo, even), jnp.where(c == 0, halo, odd)]
    for s in (1, 3, 2):
        rows += moved[s]
    stats = lax.all_to_all(stats, both, 0, 0, tiled=True).reshape(NR, NC, 4, CB)

    table = jnp.array(
        [[0, 1, 1, 1, 0, 0], [1, 1, 0, 0, 0, 1], [1, 0, 0, 0, 1, 1], [0, 0, 1, 1, 1, 0]], F32
    )
    order = ids(0, 3, 1, 2)
    w2 = run_prep(order, table[c], second_weight)
    valid = jnp.stack(
        [
            jnp.where((c == 3) & (r == NR - 1), 0.0, 1.0),
            jnp.where((c == 0) & (r == 0), 0.0, 1.0),
        ]
    ).astype(F32)
    out = run_conv2(order, valid, rows, stats, w2, out_bias[None])
    return out[:, None]


def solution(mesh):
    return jax.shard_map(
        shards,
        mesh=mesh,
        in_specs=(P(None, "rows", None, "ch"), P(None, "ch", None), P("ch"), P("ch"), P(), P()),
        out_specs=P(None, ("rows", "ch"), None, None),
        check_vma=False,
    )
```

```python
import functools
import jax
import jax.numpy as jnp
from jax import lax
from jax.experimental import pallas as pl
from jax.experimental.pallas import tpu as pltpu
from jax.sharding import PartitionSpec as P


EPS = 1e-6
F32 = jnp.float32
BF16 = jnp.bfloat16
T, Q, CB, GW = 4, 160, 128, 16
NR, NC = 32, 4


def split(v):
    hi = v.astype(BF16)
    return hi, (v - hi.astype(F32)).astype(BF16)


def time_inputs(x0, x1, x2, x3):
    return (x0, (x1 + x2) * 0.5, x1 - x0, x1 - x3, x0 - x2, (x2 - x1) * 0.5)


def time_weights(a, b, c):
    ac = a + c
    return (ac + b, c, a, ac - b)


def time_outputs(s0, s1, c0, c1, a, d):
    return (s0, s0 + c0, a + s1 + d, s1 - d - c1)


def shifted(v, by):
    rows = v.shape[0]
    rolled = pltpu.roll(v, by % rows, axis=0)
    q = lax.broadcasted_iota(jnp.int32, v.shape, 0)
    return jnp.where(q == (0 if by > 0 else rows - 1), 0.0, rolled)


def intake(lat, here, head, tail, sems):
    copies = [
        pltpu.make_async_copy(lat, here, sems.at[0]),
        pltpu.make_async_copy(lat.at[:, 0:1], head, sems.at[1]),
        pltpu.make_async_copy(lat.at[:, 1:2], tail, sems.at[2]),
    ]
    for copy in copies:
        copy.start()
    for copy in copies:
        copy.wait()


def fill_row(x, row, get):
    for f, v in enumerate(time_inputs(*(get(t) for t in range(T)))):
        for j in range(3):
            hi, lo = split(v if j == 1 else shifted(v, 1 - j))
            x[f, row, :, j * 256 : j * 256 + 128] = hi
            x[f, row, :, j * 256 + 128 : j * 256 + 256] = lo


def fill_b(w, b):
    def step(k, carry):
        i, j = k // 3, k % 3
        for m, v in enumerate(time_weights(w[k], w[9 + k], w[18 + k])):
            hi, lo = split(v)
            for half in range(2):
                at = pl.ds(pl.multiple_of(j * 256 + half * 128, 128), 128)
                b[m, i, at, 0:128] = hi
                b[m, i, at, 128:256] = lo
        return carry

    lax.fori_loop(0, 9, step, 0)


def products(x, b, p):
    for m, at, n in ((0, 0, 2), (1, 2, 2), (2, 4, 1), (3, 5, 1)):
        total = None
        for i in range(3):
            lhs = x[at : at + n, i : i + 2].reshape(n * 2 * Q, 768)
            term = jnp.dot(lhs, b[m, i], preferred_element_type=F32)
            total = term if total is None else total + term
        p[at : at + n] = halves(total, n)


def halves(v, n):
    return (v[:, :128] + v[:, 128:]).reshape(n, -1, Q, CB)


def local_products(x, b, p):
    for m, at, n in ((0, 0, 2), (1, 2, 2), (2, 4, 1), (3, 5, 1)):
        frames = slice(at, at + n)
        mid = jnp.dot(x[frames, 1:3].reshape(n * 2 * Q, 768), b[m, 1], preferred_element_type=F32)
        p[frames] = halves(mid, n)
        for out_row, in_row, i in ((0, 2, 2), (1, 1, 0)):
            side = jnp.dot(x[frames, in_row].reshape(n * Q, 768), b[m, i], preferred_element_type=F32)
            p[frames, out_row] += halves(side, n)[:, 0]


def edge_products(x, b, before, p):
    for m, at, n in ((0, 0, 2), (1, 2, 2), (2, 4, 1), (3, 5, 1)):
        frames = slice(at, at + n)
        for out_row, in_row, i in ((0, 0, 0), (1, 3, 2)):
            side = jnp.dot(x[frames, in_row].reshape(n * Q, 768), b[m, i], preferred_element_type=F32)
            p[frames, out_row] = before[frames, out_row] + halves(side, n)[:, 0]


def store_chunk(p, lo, hi):
    y = time_outputs(*(p[f] for f in range(6)))
    for t in range(T):
        ref = lo if t < 2 else hi
        ref[t % 2] = y[t]


def conv1_local(ids, lat, w, x, p, b, w1, w2, w3, w0, sems):
    copies = []
    for k, to in enumerate((w0, w1, w2, w3)):
        lanes = pl.ds(pl.multiple_of(ids[k] * CB, CB), CB)
        copies.append(pltpu.make_async_copy(w.at[:, :, lanes], to, sems.at[k]))
        copies[k].start()

    def row(k, carry):
        fill_row(x, k + 1, lambda t: lat[t, k])
        return carry

    lax.fori_loop(0, 2, row, 0)
    copies[0].wait()
    fill_b(w0, b)
    local_products(x, b, p)
    for copy in copies[1:]:
        copy.wait()


def conv1_edge(top, bot, x_in, before, b, lo, hi, x, p):
    fill_row(x, 0, lambda t: top[t, 0])
    fill_row(x, 3, lambda t: bot[t, 0])
    edge_products(x, b, before, p)
    store_chunk(p, lo, hi)


def conv1_more(n, x, *refs):
    b, p = refs[3 * n :]
    for k in range(n):
        fill_b(refs[k], b)
        products(x, b, p)
        store_chunk(p, refs[n + 2 * k], refs[n + 2 * k + 1])


HALF = jax.ShapeDtypeStruct((2, 2, Q, CB), F32)
XS = (6, 4, Q, 768)
BS, PS = (4, 3, 768, 256), (6, 2, Q, CB)
CONV1_SCRATCH = [pltpu.VMEM(BS, BF16), pltpu.VMEM(PS, F32)]
INV = pl.BlockSpec(memory_space=pltpu.VMEM)
INS = pl.BlockSpec(memory_space=pltpu.SMEM)
INH = pl.BlockSpec(memory_space=pltpu.HBM)
MB = 1024 * 1024


def run_intake(lat):
    row = jax.ShapeDtypeStruct((T, 1, Q, CB), F32)
    return pl.pallas_call(
        intake,
        in_specs=[INH],
        out_specs=[INV] * 3,
        scratch_shapes=[pltpu.SemaphoreType.DMA((3,))],
        out_shape=[jax.ShapeDtypeStruct(lat.shape, F32), row, row],
        compiler_params=pltpu.CompilerParams(vmem_limit_bytes=4 * MB),
        cost_estimate=pl.CostEstimate(flops=0, bytes_accessed=2_000_000, transcendentals=0),
        name="intake",
    )(pltpu.with_memory_space_constraint(lat, pltpu.HBM))


def run_conv1_local(ids, lat, w):
    block = jax.ShapeDtypeStruct((27, CB, CB), F32)
    return pl.pallas_call(
        conv1_local,
        in_specs=[INS, INV, INH],
        out_specs=[INV] * 6,
        scratch_shapes=[pltpu.VMEM(block.shape, F32), pltpu.SemaphoreType.DMA((4,))],
        out_shape=[jax.ShapeDtypeStruct(XS, BF16), jax.ShapeDtypeStruct(PS, F32), jax.ShapeDtypeStruct(BS, BF16)]
        + [block] * 3,
        compiler_params=pltpu.CompilerParams(vmem_limit_bytes=10 * MB),
        cost_estimate=pl.CostEstimate(flops=3_000_000_000, bytes_accessed=7_000_000, transcendentals=0),
        name="conv1_local",
    )(ids, lat, pltpu.with_memory_space_constraint(w, pltpu.HBM))


def run_conv1_edge(top, bot, x, before, b):
    return pl.pallas_call(
        conv1_edge,
        in_specs=[INV] * 5,
        out_specs=[INV] * 3,
        scratch_shapes=[pltpu.VMEM(PS, F32)],
        out_shape=[HALF, HALF, jax.ShapeDtypeStruct(XS, BF16)],
        input_output_aliases={2: 2},
        compiler_params=pltpu.CompilerParams(vmem_limit_bytes=10 * MB),
        cost_estimate=pl.CostEstimate(flops=1_500_000_000, bytes_accessed=1_000_000, transcendentals=0),
        name="conv1_edge",
    )(top, bot, x, before, b)


def run_conv1_more(x, *blocks):
    n = len(blocks)
    return pl.pallas_call(
        functools.partial(conv1_more, n),
        in_specs=[INV] * (n + 1),
        out_specs=[INV] * (2 * n),
        scratch_shapes=CONV1_SCRATCH,
        out_shape=[HALF] * (2 * n),
        compiler_params=pltpu.CompilerParams(vmem_limit_bytes=12 * MB),
        cost_estimate=pl.CostEstimate(flops=4_500_000_000 * n, bytes_accessed=2_000_000 * n, transcendentals=0),
        name="conv1_more",
    )(x, *blocks)


def group_sum(v):
    same = (
        lax.broadcasted_iota(jnp.int32, (CB, CB), 0) // GW
        == lax.broadcasted_iota(jnp.int32, (CB, CB), 1) // GW
    ).astype(F32)
    wide = jnp.broadcast_to(v, (8, CB))
    return jnp.dot(wide, same, precision=lax.Precision.HIGHEST, preferred_element_type=F32)[:1]


def finish_first(own_lo, own_hi, a1, a2, b1, b2, gain, shift, even, odd, stats):
    total = jnp.zeros((8, CB), F32)
    for t in range(T):
        own, u, v = (own_lo, a1, a2) if t < 2 else (own_hi, b1, b2)
        for k, out in enumerate((even, odd)):
            y = own[t % 2, k] + u[t % 2, k] + v[t % 2, k]
            out[t] = y
            total = total + y.reshape(Q // 8, 8, CB).sum(0)
    count = float(T * 2 * Q * GW)
    mean = group_sum(total.sum(0, keepdims=True)) / count
    square = jnp.zeros((8, CB), F32)
    for t in range(T):
        for out in (even, odd):
            d = out[t] - mean
            square = square + (d * d).reshape(Q // 8, 8, CB).sum(0)
    m2 = group_sum(square.sum(0, keepdims=True))
    row = jnp.concatenate([mean, m2, gain[...], shift[...]], axis=0)
    stats[...] = jnp.broadcast_to(row[None], stats.shape)


def run_finish(own_lo, own_hi, a1, a2, b1, b2, gain, shift):
    plane = jax.ShapeDtypeStruct((T, Q, CB), F32)
    return pl.pallas_call(
        finish_first,
        out_shape=[plane, plane, jax.ShapeDtypeStruct((NR * NC, 4, CB), F32)],
        in_specs=[INV] * 8,
        out_specs=[INV] * 3,
        compiler_params=pltpu.CompilerParams(vmem_limit_bytes=8 * MB),
        cost_estimate=pl.CostEstimate(flops=2_000_000, bytes_accessed=3_000_000, transcendentals=0),
        name="finish_first",
    )(own_lo, own_hi, a1, a2, b1, b2, gain, shift)


def prep_second(ids, sides, w, out, buf, done, sems):
    def fetch(k):
        at = pl.ds(pl.multiple_of(ids[k] * CB, CB), CB)
        return pltpu.make_async_copy(w.at[:, at, :], buf.at[k % 2], sems.at[k % 2])

    def flush(k):
        return pltpu.make_async_copy(done.at[k % 2], out.at[k], sems.at[2 + k % 2])

    fetch(0).start()
    for block in range(4):
        if block < 3:
            fetch(block + 1).start()
        if block > 1:
            flush(block - 2).wait()
        fetch(block).wait()
        taps_of, to = buf.at[block % 2], done.at[block % 2]

        def build(even_plane):
            def step(k, carry):
                rows = pl.ds(pl.multiple_of(k * 16, 16), 16)
                for side in range(2):
                    taps = []
                    for t in range(3):
                        merged = []
                        for j in range(3):
                            near, mid, far = (taps_of.at[9 * t + 3 * i + j] for i in range(3))
                            if side == 0:
                                g = near[rows, :] if even_plane else near[rows, :] + mid[rows, :]
                            else:
                                g = far[rows, :] + mid[rows, :] if even_plane else far[rows, :]
                            merged.append(g)
                        taps.append((merged[0] + merged[1] + merged[2], merged[0], merged[2]))
                    offset = sides[1 + side] * 128 + k * 16
                    dst = pl.ds(pl.multiple_of(offset, 16), 16)
                    for v in range(3):
                        for m, value in enumerate(time_weights(taps[0][v], taps[1][v], taps[2][v])):
                            hi, lo = split(value)
                            to[m, v, 0, dst, :] = hi
                            to[m, v, 1, dst, :] = lo
                return carry

            lax.fori_loop(0, 8, step, 0)

        @pl.when(sides[0] == 0)
        def _():
            build(True)

        @pl.when(sides[0] == 1)
        def _():
            build(False)

        flush(block).start()
    flush(2).wait()
    flush(3).wait()


W2S = (4, 4, 3, 2, 256, 256)


def run_prep(ids, sides, w):
    return pl.pallas_call(
        prep_second,
        in_specs=[INS, INS, INH],
        out_specs=INH,
        scratch_shapes=[
            pltpu.VMEM((2, 27, CB, 256), F32),
            pltpu.VMEM((2,) + W2S[1:], BF16),
            pltpu.SemaphoreType.DMA((4,)),
        ],
        out_shape=pltpu.HBM(W2S, BF16),
        compiler_params=pltpu.CompilerParams(vmem_limit_bytes=18 * MB),
        cost_estimate=pl.CostEstimate(flops=1_000_000, bytes_accessed=4_000_000, transcendentals=0),
        name="prep_second",
    )(ids, sides, pltpu.with_memory_space_constraint(w, pltpu.HBM))


def norm_silu(ids, k, valid, pair, stats, h):
    block = ids[k]
    count = float(T * 2 * Q * GW)
    means = stats[:, block, 0, :]
    mean = means.sum(0, keepdims=True) / NR
    off = means - mean
    m2 = stats[:, block, 1, :].sum(0, keepdims=True) + count * (off * off).sum(0, keepdims=True)
    scale = stats[0, block, 2:3, :] / jnp.sqrt(m2 / (count * NR) + EPS)
    shift = stats[0, block, 3:4, :]

    def norm(t, carry):
        for side in range(2):
            v = (pair[side][t] - mean) * scale + shift
            v = v / (1.0 + jnp.exp(-v))
            h[t, :, side * 128 : side * 128 + 128] = v * valid[side]
        return carry

    lax.fori_loop(0, T, norm, 0)


def fill_a(h, a):
    def fill(side, carry):
        lanes = pl.ds(pl.multiple_of(side * 128, 128), 128)
        x = time_inputs(*(h[t, :, lanes] for t in range(T)))
        for f in range(6):
            for v, value in enumerate((x[f], shifted(x[f], 1) - x[f], shifted(x[f], -1) - x[f])):
                hi, lo = split(value)
                a[v, 0, f, :, lanes] = hi
                a[v, 1, f, :, lanes] = lo
        return carry

    lax.fori_loop(0, 2, fill, 0)


def multiply_second(a, w, before, acc):
    def multiply(v, carry):
        for m, at, n in ((0, 0, 2), (1, 2, 2), (2, 4, 1), (3, 5, 1)):
            both = a[v, :, at : at + n].reshape(2 * n * Q, 256)
            high = jnp.dot(both, w[m, v, 0], preferred_element_type=F32)
            low = jnp.dot(
                a[v, 0, at : at + n].reshape(n * Q, 256), w[m, v, 1], preferred_element_type=F32
            )
            new = (high[: n * Q] + high[n * Q :] + low).reshape(n, Q, 256)
            acc[v, at : at + n] = new if before is None else before[v, at : at + n] + new
        return carry

    lax.fori_loop(0, 3, multiply, 0)


def conv2_most(ids, valid, e0, o0, e1, o1, e2, o2, stats, w, acc, h, a, wbuf, sems):
    def fetch(k):
        return pltpu.make_async_copy(w.at[k], wbuf.at[k % 2], sems.at[k % 2])

    fetch(0).start()
    for k, pair in enumerate(((e0, o0), (e1, o1), (e2, o2))):
        if k < 2:
            fetch(k + 1).start()
        norm_silu(ids, k, valid, pair, stats, h)
        fill_a(h, a)
        fetch(k).wait()
        multiply_second(a, wbuf.at[k % 2], acc if k else None, acc)


def conv2_last(ids, valid, e3, o3, stats, w, before, bias, out, h, a, wbuf, sems, acc, fine):
    fetch = pltpu.make_async_copy(w.at[3], wbuf.at[0], sems.at[0])
    fetch.start()
    norm_silu(ids, 3, valid, (e3, o3), stats, h)
    fill_a(h, a)
    fetch.wait()
    multiply_second(a, wbuf.at[0], before, acc)
    for half in range(2):
        lanes = slice(half * 128, half * 128 + 128)
        y = time_outputs(*(acc[0, f, :, lanes] for f in range(6)))
        for v in (1, 2):
            z = time_outputs(*(acc[v, f, :, lanes] for f in range(6)))
            for t in range(T):
                fine[t, pl.ds(v - 1, Q, stride=2), :] = y[t] + z[t] + bias[:, lanes]
        out[:, :, lanes] = fine[...]


SUMS = (3, 6, Q, 256)
CONV2_SCRATCH = [
    pltpu.VMEM((T, Q, 256), F32),
    pltpu.VMEM((3, 2, 6, Q, 256), BF16),
    pltpu.VMEM((2,) + W2S[1:], BF16),
    pltpu.SemaphoreType.DMA((2,)),
]


def run_conv2_most(ids, valid, rows, stats, w):
    return pl.pallas_call(
        conv2_most,
        in_specs=[INS, INS] + [INV] * 7 + [INH],
        out_specs=INV,
        scratch_shapes=CONV2_SCRATCH,
        out_shape=jax.ShapeDtypeStruct(SUMS, F32),
        compiler_params=pltpu.CompilerParams(vmem_limit_bytes=14 * MB),
        cost_estimate=pl.CostEstimate(flops=7_000_000_000, bytes_accessed=1_000_000, transcendentals=700_000),
        name="conv2_most",
    )(ids, valid, *rows, stats, pltpu.with_memory_space_constraint(w, pltpu.HBM))


def run_conv2_last(ids, valid, rows, stats, w, before, bias):
    return pl.pallas_call(
        conv2_last,
        in_specs=[INS, INS] + [INV] * 3 + [INH] + [INV] * 2,
        out_specs=INV,
        scratch_shapes=CONV2_SCRATCH + [pltpu.VMEM(SUMS, F32), pltpu.VMEM((T, 2 * Q, 128), F32)],
        out_shape=jax.ShapeDtypeStruct((T, 2 * Q, 256), F32),
        compiler_params=pltpu.CompilerParams(vmem_limit_bytes=18 * MB),
        cost_estimate=pl.CostEstimate(flops=2_300_000_000, bytes_accessed=1_000_000, transcendentals=200_000),
        name="conv2_last",
    )(ids, valid, *rows, stats, pltpu.with_memory_space_constraint(w, pltpu.HBM), before, bias)


def index(r, c):
    return r * NC + c


def holder(r, q, odd):
    if odd and q == 0:
        r += 1
    if not odd and q == 3:
        r -= 1
    return index(r % NR, q)


def row_perm(step, odd, hops):
    pairs = []
    for r in range(NR):
        for p in range(NC):
            a, b = (p + step * (hops - 1)) % NC, (p + step * hops) % NC
            source = index(r, p) if hops == 1 else holder(r, a, odd)
            pairs.append((source, holder(r, b, odd)))
    return pairs


def block(latent, first_weight, norm_gain, norm_shift, second_weight, out_bias):
    c = lax.axis_index("ch")
    r = lax.axis_index("rows")
    both = ("rows", "ch")
    here, head, tail = run_intake(latent)
    top = lax.ppermute(tail, "rows", [(i, i + 1) for i in range(NR - 1)])
    bot = lax.ppermute(head, "rows", [(i + 1, i) for i in range(NR - 1)])

    def ids(*shifts):
        return jnp.stack([(c + s) % NC for s in shifts]).astype(jnp.int32)

    up = [(i, (i + 1) % NC) for i in range(NC)]
    down = [((i + 1) % NC, i) for i in range(NC)]

    def send(v, perm):
        return lax.ppermute(v, "ch", perm)

    x, part, b, w1, w3, w0 = run_conv1_local(ids(2, 1, 3, 0), here, first_weight)
    far_lo, far_hi, x = run_conv1_edge(top, bot, x, part, b)
    got_lo, got_hi = send(far_lo, up), send(far_hi, down)
    up_lo, up_hi, down_lo, down_hi = run_conv1_more(x, w1, w3)
    b1, a1 = send(up_hi, up), send(down_lo, down)
    sum_lo, sum_hi = up_lo + got_lo, down_hi + got_hi
    a2, b2 = send(sum_lo, up), send(sum_hi, down)
    own_lo, own_hi = run_conv1_more(x, w0)

    order = ids(0, 3, 1, 2)
    near = jnp.where((c == 0) | (c == 3), 1, 0)
    sides = jnp.stack([c % 2, near, 1 - near]).astype(jnp.int32)
    tied, _ = lax.optimization_barrier((second_weight, sum_hi))
    w2 = run_prep(order, sides, tied)
    own_lo, w2 = lax.optimization_barrier((own_lo, w2))
    even, odd, stats = run_finish(
        own_lo, own_hi, a1, a2, b1, b2, norm_gain[None], norm_shift[None]
    )

    def move(v, step, is_odd, hops):
        return lax.ppermute(v, both, row_perm(step, is_odd, hops))

    e1, o3 = move(even, 1, False, 1), move(odd, -1, True, 1)
    o1, e3 = move(odd, 1, True, 1), move(even, -1, False, 1)
    edge = [(index(i, 0), index(i + 1, 0)) for i in range(NR - 1)]
    edge += [(index(i + 1, 3), index(i, 3)) for i in range(NR - 1)]
    stats = lax.all_to_all(stats, both, 0, 0, tiled=True).reshape(NR, NC, 4, CB)
    e2, o2 = move(e1, 1, False, 2), move(o3, -1, True, 2)
    halo = lax.ppermute(jnp.where(c == 0, odd, even), both, edge)
    e0, o0 = jnp.where(c == 3, halo, even), jnp.where(c == 0, halo, odd)

    valid = jnp.stack(
        [
            jnp.where((c == 3) & (r == NR - 1), 0.0, 1.0),
            jnp.where((c == 0) & (r == 0), 0.0, 1.0),
        ]
    ).astype(F32)
    sums = run_conv2_most(order, valid, (e0, o0, e1, o1, e3, o3), stats, w2)
    out = run_conv2_last(order, valid, (e2, o2), stats, w2, sums, out_bias[None])
    return out[:, None]


def solution(mesh):
    return jax.shard_map(
        block,
        mesh=mesh,
        in_specs=(P(None, "rows", None, "ch"), P(None, "ch", None), P("ch"), P("ch"), P(), P()),
        out_specs=P(None, ("rows", "ch"), None, None),
        check_vma=False,
    )
```

```python
import functools
import jax
import jax.numpy as jnp
from jax import lax
from jax.experimental import pallas as pl
from jax.experimental.pallas import tpu as pltpu
from jax.sharding import PartitionSpec as P


EPS = 1e-6
F32 = jnp.float32
BF16 = jnp.bfloat16
T, Q, CB, GW = 4, 160, 128, 16
NR, NC = 32, 4


def split(v):
    hi = v.astype(BF16)
    return hi, (v - hi.astype(F32)).astype(BF16)


def time_inputs(x0, x1, x2, x3):
    return (x0, (x1 + x2) * 0.5, x1 - x0, x1 - x3, x0 - x2, (x2 - x1) * 0.5)


def time_weights(a, b, c):
    ac = a + c
    return (ac + b, c, a, ac - b)


def time_outputs(s0, s1, c0, c1, a, d):
    return (s0, s0 + c0, a + s1 + d, s1 - d - c1)


def shifted(v, by):
    rows = v.shape[0]
    rolled = pltpu.roll(v, by % rows, axis=0)
    q = lax.broadcasted_iota(jnp.int32, v.shape, 0)
    return jnp.where(q == (0 if by > 0 else rows - 1), 0.0, rolled)


def intake(lat, here, head, tail, sems):
    copies = [
        pltpu.make_async_copy(lat, here, sems.at[0]),
        pltpu.make_async_copy(lat.at[:, 0:1], head, sems.at[1]),
        pltpu.make_async_copy(lat.at[:, 1:2], tail, sems.at[2]),
    ]
    for copy in copies:
        copy.start()
    for copy in copies:
        copy.wait()


def fill_row(x, row, get):
    for f, v in enumerate(time_inputs(*(get(t) for t in range(T)))):
        for j in range(3):
            hi, lo = split(v if j == 1 else shifted(v, 1 - j))
            x[f, row, :, j * 256 : j * 256 + 128] = hi
            x[f, row, :, j * 256 + 128 : j * 256 + 256] = lo


def fill_b(w, b):
    def step(k, carry):
        i, j = k // 3, k % 3
        for m, v in enumerate(time_weights(w[k], w[9 + k], w[18 + k])):
            hi, lo = split(v)
            for half in range(2):
                at = pl.ds(pl.multiple_of(j * 256 + half * 128, 128), 128)
                b[m, i, at, 0:128] = hi
                b[m, i, at, 128:256] = lo
        return carry

    lax.fori_loop(0, 9, step, 0)


def products(x, b, p):
    for m, at, n in ((0, 0, 2), (1, 2, 2), (2, 4, 1), (3, 5, 1)):
        total = None
        for i in range(3):
            lhs = x[at : at + n, i : i + 2].reshape(n * 2 * Q, 768)
            term = jnp.dot(lhs, b[m, i], preferred_element_type=F32)
            total = term if total is None else total + term
        p[at : at + n] = halves(total, n)


def halves(v, n):
    return (v[:, :128] + v[:, 128:]).reshape(n, -1, Q, CB)


def local_products(x, b, p):
    for m, at, n in ((0, 0, 2), (1, 2, 2), (2, 4, 1), (3, 5, 1)):
        frames = slice(at, at + n)
        mid = jnp.dot(x[frames, 1:3].reshape(n * 2 * Q, 768), b[m, 1], preferred_element_type=F32)
        p[frames] = halves(mid, n)
        for out_row, in_row, i in ((0, 2, 2), (1, 1, 0)):
            side = jnp.dot(x[frames, in_row].reshape(n * Q, 768), b[m, i], preferred_element_type=F32)
            p[frames, out_row] += halves(side, n)[:, 0]


def edge_products(x, b, before, p):
    for m, at, n in ((0, 0, 2), (1, 2, 2), (2, 4, 1), (3, 5, 1)):
        frames = slice(at, at + n)
        for out_row, in_row, i in ((0, 0, 0), (1, 3, 2)):
            side = jnp.dot(x[frames, in_row].reshape(n * Q, 768), b[m, i], preferred_element_type=F32)
            p[frames, out_row] = before[frames, out_row] + halves(side, n)[:, 0]


def store_chunk(p, lo, hi):
    y = time_outputs(*(p[f] for f in range(6)))
    for t in range(T):
        ref = lo if t < 2 else hi
        ref[t % 2] = y[t]


def conv1_local(ids, lat, w, x, p, b, w1, w2, w3, w0, sems):
    copies = []
    for k, to in enumerate((w0, w1, w2, w3)):
        lanes = pl.ds(pl.multiple_of(ids[k] * CB, CB), CB)
        copies.append(pltpu.make_async_copy(w.at[:, :, lanes], to, sems.at[k]))
        copies[k].start()

    def row(k, carry):
        fill_row(x, k + 1, lambda t: lat[t, k])
        return carry

    lax.fori_loop(0, 2, row, 0)
    copies[0].wait()
    fill_b(w0, b)
    local_products(x, b, p)
    for copy in copies[1:]:
        copy.wait()


def conv1_edge(top, bot, x_in, before, b, lo, hi, x, p):
    fill_row(x, 0, lambda t: top[t, 0])
    fill_row(x, 3, lambda t: bot[t, 0])
    edge_products(x, b, before, p)
    store_chunk(p, lo, hi)


def conv1_more(n, x, *refs):
    b, p = refs[3 * n :]
    for k in range(n):
        fill_b(refs[k], b)
        products(x, b, p)
        store_chunk(p, refs[n + 2 * k], refs[n + 2 * k + 1])


def conv1_near(ids, x, w1, w3, w2, *refs):
    outs, taps, (b, p, sems) = refs[:4], refs[4:8], refs[8:]
    copies = []
    for k in range(4):
        at = pl.ds(pl.multiple_of(ids[k] * CB, CB), CB)
        copies.append(pltpu.make_async_copy(w2.at[:, at, :], taps[k], sems.at[k]))
        copies[k].start()
    conv1_more(2, x, w1, w3, *outs, b, p)
    for copy in copies:
        copy.wait()


HALF = jax.ShapeDtypeStruct((2, 2, Q, CB), F32)
XS = (6, 4, Q, 768)
BS, PS = (4, 3, 768, 256), (6, 2, Q, CB)
CONV1_SCRATCH = [pltpu.VMEM(BS, BF16), pltpu.VMEM(PS, F32)]
INV = pl.BlockSpec(memory_space=pltpu.VMEM)
INS = pl.BlockSpec(memory_space=pltpu.SMEM)
INH = pl.BlockSpec(memory_space=pltpu.HBM)
MB = 1024 * 1024


def run_intake(lat):
    row = jax.ShapeDtypeStruct((T, 1, Q, CB), F32)
    return pl.pallas_call(
        intake,
        in_specs=[INH],
        out_specs=[INV] * 3,
        scratch_shapes=[pltpu.SemaphoreType.DMA((3,))],
        out_shape=[jax.ShapeDtypeStruct(lat.shape, F32), row, row],
        compiler_params=pltpu.CompilerParams(vmem_limit_bytes=4 * MB),
        cost_estimate=pl.CostEstimate(flops=0, bytes_accessed=2_000_000, transcendentals=0),
        name="intake",
    )(pltpu.with_memory_space_constraint(lat, pltpu.HBM))


def run_conv1_local(ids, lat, w):
    block = jax.ShapeDtypeStruct((27, CB, CB), F32)
    return pl.pallas_call(
        conv1_local,
        in_specs=[INS, INV, INH],
        out_specs=[INV] * 6,
        scratch_shapes=[pltpu.VMEM(block.shape, F32), pltpu.SemaphoreType.DMA((4,))],
        out_shape=[jax.ShapeDtypeStruct(XS, BF16), jax.ShapeDtypeStruct(PS, F32), jax.ShapeDtypeStruct(BS, BF16)]
        + [block] * 3,
        compiler_params=pltpu.CompilerParams(vmem_limit_bytes=10 * MB),
        cost_estimate=pl.CostEstimate(flops=3_000_000_000, bytes_accessed=7_000_000, transcendentals=0),
        name="conv1_local",
    )(ids, lat, pltpu.with_memory_space_constraint(w, pltpu.HBM))


def run_conv1_edge(top, bot, x, before, b):
    return pl.pallas_call(
        conv1_edge,
        in_specs=[INV] * 5,
        out_specs=[INV] * 3,
        scratch_shapes=[pltpu.VMEM(PS, F32)],
        out_shape=[HALF, HALF, jax.ShapeDtypeStruct(XS, BF16)],
        input_output_aliases={2: 2},
        compiler_params=pltpu.CompilerParams(vmem_limit_bytes=10 * MB),
        cost_estimate=pl.CostEstimate(flops=1_500_000_000, bytes_accessed=1_000_000, transcendentals=0),
        name="conv1_edge",
    )(top, bot, x, before, b)


def run_conv1_more(x, *blocks):
    n = len(blocks)
    return pl.pallas_call(
        functools.partial(conv1_more, n),
        in_specs=[INV] * (n + 1),
        out_specs=[INV] * (2 * n),
        scratch_shapes=CONV1_SCRATCH,
        out_shape=[HALF] * (2 * n),
        compiler_params=pltpu.CompilerParams(vmem_limit_bytes=10 * MB),
        cost_estimate=pl.CostEstimate(flops=4_500_000_000 * n, bytes_accessed=2_000_000 * n, transcendentals=0),
        name="conv1_more",
    )(x, *blocks)


def run_conv1_near(ids, x, w1, w3, w2):
    return pl.pallas_call(
        conv1_near,
        in_specs=[INS] + [INV] * 3 + [INH],
        out_specs=[INV] * 8,
        scratch_shapes=CONV1_SCRATCH + [pltpu.SemaphoreType.DMA((4,))],
        out_shape=[HALF] * 4 + [jax.ShapeDtypeStruct((27, CB, 256), F32)] * 4,
        compiler_params=pltpu.CompilerParams(vmem_limit_bytes=10 * MB),
        cost_estimate=pl.CostEstimate(flops=9_000_000_000, bytes_accessed=16_000_000, transcendentals=0),
        name="conv1_near",
    )(ids, x, w1, w3, pltpu.with_memory_space_constraint(w2, pltpu.HBM))


def group_sum(v):
    same = (
        lax.broadcasted_iota(jnp.int32, (CB, CB), 0) // GW
        == lax.broadcasted_iota(jnp.int32, (CB, CB), 1) // GW
    ).astype(F32)
    wide = jnp.broadcast_to(v, (8, CB))
    return jnp.dot(wide, same, precision=lax.Precision.HIGHEST, preferred_element_type=F32)[:1]


def finish_first(plane, own_lo, own_hi, a1, a2, b1, b2, gain, shift, even, odd, edge, stats):
    total = jnp.zeros((8, CB), F32)
    for t in range(T):
        own, u, v = (own_lo, a1, a2) if t < 2 else (own_hi, b1, b2)
        for k, out in enumerate((even, odd)):
            y = own[t % 2, k] + u[t % 2, k] + v[t % 2, k]
            out[t] = y
            total = total + y.reshape(Q // 8, 8, CB).sum(0)
    count = float(T * 2 * Q * GW)
    mean = group_sum(total.sum(0, keepdims=True)) / count
    square = jnp.zeros((8, CB), F32)
    for t in range(T):
        edge[t] = jnp.where(plane[0] == 0, odd[t], even[t])
        for out in (even, odd):
            d = out[t] - mean
            square = square + (d * d).reshape(Q // 8, 8, CB).sum(0)
    m2 = group_sum(square.sum(0, keepdims=True))
    row = jnp.concatenate([mean, m2, gain[...], shift[...]], axis=0)
    stats[...] = jnp.broadcast_to(row[None], stats.shape)


def run_finish(plane_id, own_lo, own_hi, a1, a2, b1, b2, gain, shift):
    plane = jax.ShapeDtypeStruct((T, Q, CB), F32)
    return pl.pallas_call(
        finish_first,
        out_shape=[plane, plane, plane, jax.ShapeDtypeStruct((NR * NC, 4, CB), F32)],
        in_specs=[INS] + [INV] * 8,
        out_specs=[INV] * 4,
        compiler_params=pltpu.CompilerParams(vmem_limit_bytes=8 * MB),
        cost_estimate=pl.CostEstimate(flops=2_000_000, bytes_accessed=3_000_000, transcendentals=0),
        name="finish_first",
    )(plane_id, own_lo, own_hi, a1, a2, b1, b2, gain, shift)


def prep_second(sides, *refs):
    blocks, (out, done, sems) = refs[:4], refs[4:]

    def flush(k):
        return pltpu.make_async_copy(done.at[k % 2], out.at[k], sems.at[k % 2])

    for block in range(4):
        if block > 1:
            flush(block - 2).wait()
        taps_of, to = blocks[block], done.at[block % 2]

        def build(even_plane):
            def step(k, carry):
                rows = pl.ds(pl.multiple_of(k * 16, 16), 16)
                for side in range(2):
                    taps = []
                    for t in range(3):
                        merged = []
                        for j in range(3):
                            near, mid, far = (taps_of.at[9 * t + 3 * i + j] for i in range(3))
                            if side == 0:
                                g = near[rows, :] if even_plane else near[rows, :] + mid[rows, :]
                            else:
                                g = far[rows, :] + mid[rows, :] if even_plane else far[rows, :]
                            merged.append(g)
                        taps.append((merged[0] + merged[1] + merged[2], merged[0], merged[2]))
                    offset = sides[1 + side] * 128 + k * 16
                    dst = pl.ds(pl.multiple_of(offset, 16), 16)
                    for v in range(3):
                        for m, value in enumerate(time_weights(taps[0][v], taps[1][v], taps[2][v])):
                            hi, lo = split(value)
                            to[m, v, 0, dst, :] = hi
                            to[m, v, 1, dst, :] = lo
                return carry

            lax.fori_loop(0, 8, step, 0)

        @pl.when(sides[0] == 0)
        def _():
            build(True)

        @pl.when(sides[0] == 1)
        def _():
            build(False)

        flush(block).start()
    flush(2).wait()
    flush(3).wait()


W2S = (4, 4, 3, 2, 256, 256)


def run_prep(sides, blocks):
    return pl.pallas_call(
        prep_second,
        in_specs=[INS] + [INV] * 4,
        out_specs=INH,
        scratch_shapes=[pltpu.VMEM((2,) + W2S[1:], BF16), pltpu.SemaphoreType.DMA((2,))],
        out_shape=pltpu.HBM(W2S, BF16),
        compiler_params=pltpu.CompilerParams(vmem_limit_bytes=10 * MB),
        cost_estimate=pl.CostEstimate(flops=1_000_000, bytes_accessed=4_000_000, transcendentals=0),
        name="prep_second",
    )(sides, *blocks)


def rows_of(even, odd):
    return lambda t: even[t], lambda t: odd[t]


def norm_silu(ids, k, valid, pair, stats, h):
    block = ids[k]
    count = float(T * 2 * Q * GW)
    means = stats[:, block, 0, :]
    mean = means.sum(0, keepdims=True) / NR
    off = means - mean
    m2 = stats[:, block, 1, :].sum(0, keepdims=True) + count * (off * off).sum(0, keepdims=True)
    scale = stats[0, block, 2:3, :] / jnp.sqrt(m2 / (count * NR) + EPS)
    shift = stats[0, block, 3:4, :]

    def norm(t, carry):
        for side in range(2):
            v = (pair[side](t) - mean) * scale + shift
            v = v / (1.0 + jnp.exp(-v))
            h[t, :, side * 128 : side * 128 + 128] = v * valid[side]
        return carry

    lax.fori_loop(0, T, norm, 0)


def fill_a(h, a):
    def fill(side, carry):
        lanes = pl.ds(pl.multiple_of(side * 128, 128), 128)
        x = time_inputs(*(h[t, :, lanes] for t in range(T)))
        for f in range(6):
            for v, value in enumerate((x[f], shifted(x[f], 1) - x[f], shifted(x[f], -1) - x[f])):
                hi, lo = split(value)
                a[v, 0, f, :, lanes] = hi
                a[v, 1, f, :, lanes] = lo
        return carry

    lax.fori_loop(0, 2, fill, 0)


def multiply_second(a, w, before, acc):
    for v in range(3):
        for m, at, n in ((0, 0, 2), (1, 2, 2), (2, 4, 1), (3, 5, 1)):
            hi, lo = (a[v, k, at : at + n].reshape(n * Q, 256) for k in range(2))
            new = jnp.dot(
                jnp.concatenate([hi, hi, lo], axis=1),
                jnp.concatenate([w[m, v, 0], w[m, v, 1], w[m, v, 0]], axis=0),
                preferred_element_type=F32,
            ).reshape(n, Q, 256)
            acc[v, at : at + n] = new if before is None else before[v, at : at + n] + new


def conv2_near(ids, valid, e1, o1, e2, o2, stats, w, acc, w0, w3, h, a, wbuf, sems):
    order = ((1, wbuf.at[0]), (2, wbuf.at[1]), (0, w0), (3, w3))
    fetches = [pltpu.make_async_copy(w.at[k], to, sems.at[k]) for k, to in order]
    for fetch in fetches:
        fetch.start()
    for k, pair in ((1, rows_of(e1, o1)), (2, rows_of(e2, o2))):
        norm_silu(ids, k, valid, pair, stats, h)
        fill_a(h, a)
        fetches[k - 1].wait()
        multiply_second(a, wbuf.at[k - 1], None if k == 1 else acc, acc)
    for fetch in fetches[2:]:
        fetch.wait()


def conv2_last(ids, valid, e0, o0, halo, e3, o3, stats, w0, w3, before, bias, out, h, a, acc, fine, sems):
    plane = ids[0]
    own = (
        lambda t: jnp.where(plane == 3, halo[t], e0[t]),
        lambda t: jnp.where(plane == 0, halo[t], o0[t]),
    )
    for k, pair, w in ((0, own, w0), (3, rows_of(e3, o3), w3)):
        norm_silu(ids, k, valid, pair, stats, h)
        fill_a(h, a)
        multiply_second(a, w, before if k == 0 else acc, acc)
    copies = []
    for half in range(2):
        lanes = slice(half * 128, half * 128 + 128)
        y = time_outputs(*(acc[0, f, :, lanes] for f in range(6)))
        for v in (1, 2):
            z = time_outputs(*(acc[v, f, :, lanes] for f in range(6)))
            for t in range(T):
                fine[half, t, pl.ds(v - 1, Q, stride=2), :] = y[t] + z[t] + bias[:, lanes]
        copies.append(pltpu.make_async_copy(fine.at[half], out.at[:, :, lanes], sems.at[half]))
        copies[half].start()
    for copy in copies:
        copy.wait()


SUMS = (3, 6, Q, 256)
CONV2_SCRATCH = [pltpu.VMEM((T, Q, 256), F32), pltpu.VMEM((3, 2, 6, Q, 256), BF16)]


def run_conv2_near(ids, valid, rows, stats, w):
    block = jax.ShapeDtypeStruct(W2S[1:], BF16)
    return pl.pallas_call(
        conv2_near,
        in_specs=[INS, INS] + [INV] * 5 + [INH],
        out_specs=[INV] * 3,
        scratch_shapes=CONV2_SCRATCH + [pltpu.VMEM((2,) + W2S[1:], BF16), pltpu.SemaphoreType.DMA((4,))],
        out_shape=[jax.ShapeDtypeStruct(SUMS, F32), block, block],
        compiler_params=pltpu.CompilerParams(vmem_limit_bytes=14 * MB),
        cost_estimate=pl.CostEstimate(flops=4_600_000_000, bytes_accessed=13_000_000, transcendentals=400_000),
        name="conv2_near",
    )(ids, valid, *rows, stats, pltpu.with_memory_space_constraint(w, pltpu.HBM))


def run_conv2_last(ids, valid, rows, stats, w0, w3, before, bias):
    return pl.pallas_call(
        conv2_last,
        in_specs=[INS, INS] + [INV] * 10,
        out_specs=INH,
        scratch_shapes=CONV2_SCRATCH
        + [pltpu.VMEM(SUMS, F32), pltpu.VMEM((2, T, 2 * Q, 128), F32), pltpu.SemaphoreType.DMA((2,))],
        out_shape=pltpu.HBM((T, 2 * Q, 256), F32),
        compiler_params=pltpu.CompilerParams(vmem_limit_bytes=14 * MB),
        cost_estimate=pl.CostEstimate(flops=4_600_000_000, bytes_accessed=1_000_000, transcendentals=400_000),
        name="conv2_last",
    )(ids, valid, *rows, stats, w0, w3, before, bias)


def index(r, c):
    return r * NC + c


def holder(r, q, odd):
    if odd and q == 0:
        r += 1
    if not odd and q == 3:
        r -= 1
    return index(r % NR, q)


def row_perm(step, odd, hops):
    pairs = []
    for r in range(NR):
        for p in range(NC):
            a, b = (p + step * (hops - 1)) % NC, (p + step * hops) % NC
            source = index(r, p) if hops == 1 else holder(r, a, odd)
            pairs.append((source, holder(r, b, odd)))
    return pairs


def block(latent, first_weight, norm_gain, norm_shift, second_weight, out_bias):
    c = lax.axis_index("ch")
    r = lax.axis_index("rows")
    both = ("rows", "ch")
    here, head, tail = run_intake(latent)
    top = lax.ppermute(tail, "rows", [(i, i + 1) for i in range(NR - 1)])
    bot = lax.ppermute(head, "rows", [(i + 1, i) for i in range(NR - 1)])

    def ids(*shifts):
        return jnp.stack([(c + s) % NC for s in shifts]).astype(jnp.int32)

    up = [(i, (i + 1) % NC) for i in range(NC)]
    down = [((i + 1) % NC, i) for i in range(NC)]

    def send(v, perm):
        return lax.ppermute(v, "ch", perm)

    x, part, b, w1, w3, w0 = run_conv1_local(ids(2, 1, 3, 0), here, first_weight)
    far_lo, far_hi, x = run_conv1_edge(top, bot, x, part, b)
    got_lo, got_hi = send(far_lo, up), send(far_hi, down)
    order = ids(0, 3, 1, 2)
    up_lo, up_hi, down_lo, down_hi, *blocks = run_conv1_near(order, x, w1, w3, second_weight)
    b1, a1 = send(up_hi, up), send(down_lo, down)
    sum_lo, sum_hi = up_lo + got_lo, down_hi + got_hi
    a2, b2 = send(sum_lo, up), send(sum_hi, down)
    own_lo, own_hi = run_conv1_more(x, w0)

    near = jnp.where((c == 0) | (c == 3), 1, 0)
    sides = jnp.stack([c % 2, near, 1 - near]).astype(jnp.int32)
    tied = lax.optimization_barrier((*blocks, sum_hi))
    w2 = run_prep(sides, tied[:4])
    own_lo, w2 = lax.optimization_barrier((own_lo, w2))
    even, odd, edge_row, stats = run_finish(
        c[None].astype(jnp.int32), own_lo, own_hi, a1, a2, b1, b2, norm_gain[None], norm_shift[None]
    )

    def move(v, step, is_odd, hops):
        return lax.ppermute(v, both, row_perm(step, is_odd, hops))

    e1, o3 = move(even, 1, False, 1), move(odd, -1, True, 1)
    o1, e3 = move(odd, 1, True, 1), move(even, -1, False, 1)
    edge = [(index(i, 0), index(i + 1, 0)) for i in range(NR - 1)]
    edge += [(index(i + 1, 3), index(i, 3)) for i in range(NR - 1)]
    stats = lax.all_to_all(stats, both, 0, 0, tiled=True).reshape(NR, NC, 4, CB)
    e2, o2 = move(e1, 1, False, 2), move(o3, -1, True, 2)
    halo = lax.ppermute(edge_row, both, edge)

    valid = jnp.stack(
        [
            jnp.where((c == 3) & (r == NR - 1), 0.0, 1.0),
            jnp.where((c == 0) & (r == 0), 0.0, 1.0),
        ]
    ).astype(F32)
    sums, w2_own, w2_far = run_conv2_near(order, valid, (e1, o1, e3, o3), stats, w2)
    rows = (even, odd, halo, e2, o2)
    out = run_conv2_last(order, valid, rows, stats, w2_own, w2_far, sums, out_bias[None])
    return out[:, None]


def solution(mesh):
    return jax.shard_map(
        block,
        mesh=mesh,
        in_specs=(P(None, "rows", None, "ch"), P(None, "ch", None), P("ch"), P("ch"), P(), P()),
        out_specs=P(None, ("rows", "ch"), None, None),
        check_vma=False,
    )
```

```python
import functools
import jax
import jax.numpy as jnp
from jax import lax
from jax.experimental import pallas as pl
from jax.experimental.pallas import tpu as pltpu
from jax.sharding import PartitionSpec as P


EPS = 1e-6
F32 = jnp.float32
BF16 = jnp.bfloat16
T, Q, CB, GW = 4, 160, 128, 16
NR, NC = 32, 4


def split(v):
    hi = v.astype(BF16)
    return hi, (v - hi.astype(F32)).astype(BF16)


def time_inputs(x0, x1, x2, x3):
    return (x0, (x1 + x2) * 0.5, x1 - x0, x1 - x3, x0 - x2, (x2 - x1) * 0.5)


def time_weights(a, b, c):
    ac = a + c
    return (ac + b, c, a, ac - b)


def time_outputs(s0, s1, c0, c1, a, d):
    return (s0, s0 + c0, a + s1 + d, s1 - d - c1)


def shifted(v, by):
    rows = v.shape[0]
    rolled = pltpu.roll(v, by % rows, axis=0)
    q = lax.broadcasted_iota(jnp.int32, v.shape, 0)
    return jnp.where(q == (0 if by > 0 else rows - 1), 0.0, rolled)


def intake(lat, here, head, tail, sems):
    copies = [
        pltpu.make_async_copy(lat, here, sems.at[0]),
        pltpu.make_async_copy(lat.at[:, 0:1], head, sems.at[1]),
        pltpu.make_async_copy(lat.at[:, 1:2], tail, sems.at[2]),
    ]
    for copy in copies:
        copy.start()
    for copy in copies:
        copy.wait()


def fill_row(x, row, get):
    for f, v in enumerate(time_inputs(*(get(t) for t in range(T)))):
        for j in range(3):
            hi, lo = split(v if j == 1 else shifted(v, 1 - j))
            x[f, row, :, j * 256 : j * 256 + 128] = hi
            x[f, row, :, j * 256 + 128 : j * 256 + 256] = lo


def fill_b(w, b):
    def step(k, carry):
        i, j = k // 3, k % 3
        for m, v in enumerate(time_weights(w[k], w[9 + k], w[18 + k])):
            hi, lo = split(v)
            for half in range(2):
                at = pl.ds(pl.multiple_of(j * 256 + half * 128, 128), 128)
                b[m, i, at, 0:128] = hi
                b[m, i, at, 128:256] = lo
        return carry

    lax.fori_loop(0, 9, step, 0)


def products(x, b, p):
    for m, at, n in ((0, 0, 2), (1, 2, 2), (2, 4, 1), (3, 5, 1)):
        total = None
        for i in range(3):
            lhs = x[at : at + n, i : i + 2].reshape(n * 2 * Q, 768)
            term = jnp.dot(lhs, b[m, i], preferred_element_type=F32)
            total = term if total is None else total + term
        p[at : at + n] = halves(total, n)


def halves(v, n):
    return (v[:, :128] + v[:, 128:]).reshape(n, -1, Q, CB)


def local_products(x, b, p):
    for m, at, n in ((0, 0, 2), (1, 2, 2), (2, 4, 1), (3, 5, 1)):
        frames = slice(at, at + n)
        mid = jnp.dot(x[frames, 1:3].reshape(n * 2 * Q, 768), b[m, 1], preferred_element_type=F32)
        p[frames] = halves(mid, n)
        for out_row, in_row, i in ((0, 2, 2), (1, 1, 0)):
            side = jnp.dot(x[frames, in_row].reshape(n * Q, 768), b[m, i], preferred_element_type=F32)
            p[frames, out_row] += halves(side, n)[:, 0]


def edge_products(x, b, before, p):
    for m, at, n in ((0, 0, 2), (1, 2, 2), (2, 4, 1), (3, 5, 1)):
        frames = slice(at, at + n)
        for out_row, in_row, i in ((0, 0, 0), (1, 3, 2)):
            side = jnp.dot(x[frames, in_row].reshape(n * Q, 768), b[m, i], preferred_element_type=F32)
            p[frames, out_row] = before[frames, out_row] + halves(side, n)[:, 0]


def store_chunk(p, lo, hi):
    y = time_outputs(*(p[f] for f in range(6)))
    for t in range(T):
        ref = lo if t < 2 else hi
        ref[t % 2] = y[t]


def conv1_local(ids, lat, w, x, p, b, w1, w2, w3, w0, sems):
    copies = []
    for k, to in enumerate((w0, w1, w2, w3)):
        lanes = pl.ds(pl.multiple_of(ids[k] * CB, CB), CB)
        copies.append(pltpu.make_async_copy(w.at[:, :, lanes], to, sems.at[k]))
    copies[0].start()

    def row(k, carry):
        fill_row(x, k + 1, lambda t: lat[t, k])
        return carry

    lax.fori_loop(0, 2, row, 0)
    copies[0].wait()
    for copy in copies[1:]:
        copy.start()
    fill_b(w0, b)
    local_products(x, b, p)
    for copy in copies[1:]:
        copy.wait()


def conv1_edge(top, bot, x_in, before, b, lo, hi, x, p):
    fill_row(x, 0, lambda t: top[t, 0])
    fill_row(x, 3, lambda t: bot[t, 0])
    edge_products(x, b, before, p)
    store_chunk(p, lo, hi)


def conv1_more(n, x, *refs):
    b, p = refs[3 * n :]
    for k in range(n):
        fill_b(refs[k], b)
        products(x, b, p)
        store_chunk(p, refs[n + 2 * k], refs[n + 2 * k + 1])


def conv1_near(ids, x, w1, w3, w2, *refs):
    outs, taps, (b, p, sems) = refs[:4], refs[4:8], refs[8:]
    copies = []
    for k in range(4):
        at = pl.ds(pl.multiple_of(ids[k] * CB, CB), CB)
        copies.append(pltpu.make_async_copy(w2.at[:, at, :], taps[k], sems.at[k]))
        copies[k].start()
    conv1_more(2, x, w1, w3, *outs, b, p)
    for copy in copies:
        copy.wait()


HALF = jax.ShapeDtypeStruct((2, 2, Q, CB), F32)
XS = (6, 4, Q, 768)
BS, PS = (4, 3, 768, 256), (6, 2, Q, CB)
CONV1_SCRATCH = [pltpu.VMEM(BS, BF16), pltpu.VMEM(PS, F32)]
INV = pl.BlockSpec(memory_space=pltpu.VMEM)
INS = pl.BlockSpec(memory_space=pltpu.SMEM)
INH = pl.BlockSpec(memory_space=pltpu.HBM)
MB = 1024 * 1024


def run_intake(lat):
    row = jax.ShapeDtypeStruct((T, 1, Q, CB), F32)
    return pl.pallas_call(
        intake,
        in_specs=[INH],
        out_specs=[INV] * 3,
        scratch_shapes=[pltpu.SemaphoreType.DMA((3,))],
        out_shape=[jax.ShapeDtypeStruct(lat.shape, F32), row, row],
        compiler_params=pltpu.CompilerParams(vmem_limit_bytes=4 * MB),
        cost_estimate=pl.CostEstimate(flops=0, bytes_accessed=2_000_000, transcendentals=0),
        name="intake",
    )(pltpu.with_memory_space_constraint(lat, pltpu.HBM))


def run_conv1_local(ids, lat, w):
    block = jax.ShapeDtypeStruct((27, CB, CB), F32)
    return pl.pallas_call(
        conv1_local,
        in_specs=[INS, INV, INH],
        out_specs=[INV] * 6,
        scratch_shapes=[pltpu.VMEM(block.shape, F32), pltpu.SemaphoreType.DMA((4,))],
        out_shape=[jax.ShapeDtypeStruct(XS, BF16), jax.ShapeDtypeStruct(PS, F32), jax.ShapeDtypeStruct(BS, BF16)]
        + [block] * 3,
        compiler_params=pltpu.CompilerParams(vmem_limit_bytes=10 * MB),
        cost_estimate=pl.CostEstimate(flops=3_000_000_000, bytes_accessed=7_000_000, transcendentals=0),
        name="conv1_local",
    )(ids, lat, pltpu.with_memory_space_constraint(w, pltpu.HBM))


def run_conv1_edge(top, bot, x, before, b):
    return pl.pallas_call(
        conv1_edge,
        in_specs=[INV] * 5,
        out_specs=[INV] * 3,
        scratch_shapes=[pltpu.VMEM(PS, F32)],
        out_shape=[HALF, HALF, jax.ShapeDtypeStruct(XS, BF16)],
        input_output_aliases={2: 2},
        compiler_params=pltpu.CompilerParams(vmem_limit_bytes=10 * MB),
        cost_estimate=pl.CostEstimate(flops=1_500_000_000, bytes_accessed=1_000_000, transcendentals=0),
        name="conv1_edge",
    )(top, bot, x, before, b)


def run_conv1_more(x, *blocks):
    n = len(blocks)
    return pl.pallas_call(
        functools.partial(conv1_more, n),
        in_specs=[INV] * (n + 1),
        out_specs=[INV] * (2 * n),
        scratch_shapes=CONV1_SCRATCH,
        out_shape=[HALF] * (2 * n),
        compiler_params=pltpu.CompilerParams(vmem_limit_bytes=10 * MB),
        cost_estimate=pl.CostEstimate(flops=4_500_000_000 * n, bytes_accessed=2_000_000 * n, transcendentals=0),
        name="conv1_more",
    )(x, *blocks)


def run_conv1_near(ids, x, w1, w3, w2):
    return pl.pallas_call(
        conv1_near,
        in_specs=[INS] + [INV] * 3 + [INH],
        out_specs=[INV] * 8,
        scratch_shapes=CONV1_SCRATCH + [pltpu.SemaphoreType.DMA((4,))],
        out_shape=[HALF] * 4 + [jax.ShapeDtypeStruct((27, CB, 256), F32)] * 4,
        compiler_params=pltpu.CompilerParams(vmem_limit_bytes=10 * MB),
        cost_estimate=pl.CostEstimate(flops=9_000_000_000, bytes_accessed=16_000_000, transcendentals=0),
        name="conv1_near",
    )(ids, x, w1, w3, pltpu.with_memory_space_constraint(w2, pltpu.HBM))


def group_sum(v):
    same = (
        lax.broadcasted_iota(jnp.int32, (CB, CB), 0) // GW
        == lax.broadcasted_iota(jnp.int32, (CB, CB), 1) // GW
    ).astype(F32)
    wide = jnp.broadcast_to(v, (8, CB))
    return jnp.dot(wide, same, precision=lax.Precision.HIGHEST, preferred_element_type=F32)[:1]


def finish_first(plane, own_lo, own_hi, a1, a2, b1, b2, gain, shift, even, odd, edge, stats):
    total = jnp.zeros((8, CB), F32)
    for t in range(T):
        own, u, v = (own_lo, a1, a2) if t < 2 else (own_hi, b1, b2)
        for k, out in enumerate((even, odd)):
            y = own[t % 2, k] + u[t % 2, k] + v[t % 2, k]
            out[t] = y
            total = total + y.reshape(Q // 8, 8, CB).sum(0)
    count = float(T * 2 * Q * GW)
    mean = group_sum(total.sum(0, keepdims=True)) / count
    square = jnp.zeros((8, CB), F32)
    for t in range(T):
        edge[t] = jnp.where(plane[0] == 0, odd[t], even[t])
        for out in (even, odd):
            d = out[t] - mean
            square = square + (d * d).reshape(Q // 8, 8, CB).sum(0)
    m2 = group_sum(square.sum(0, keepdims=True))
    row = jnp.concatenate([mean, m2, gain[...], shift[...]], axis=0)
    stats[...] = jnp.broadcast_to(row[None], stats.shape)


def run_finish(plane_id, own_lo, own_hi, a1, a2, b1, b2, gain, shift):
    plane = jax.ShapeDtypeStruct((T, Q, CB), F32)
    return pl.pallas_call(
        finish_first,
        out_shape=[plane, plane, plane, jax.ShapeDtypeStruct((NR * NC, 4, CB), F32)],
        in_specs=[INS] + [INV] * 8,
        out_specs=[INV] * 4,
        compiler_params=pltpu.CompilerParams(vmem_limit_bytes=8 * MB),
        cost_estimate=pl.CostEstimate(flops=2_000_000, bytes_accessed=3_000_000, transcendentals=0),
        name="finish_first",
    )(plane_id, own_lo, own_hi, a1, a2, b1, b2, gain, shift)


def prep_second(sides, *refs):
    blocks, (out, done, sems) = refs[:4], refs[4:]

    def flush(k):
        return pltpu.make_async_copy(done.at[k], out.at[k], sems.at[k])

    for block in range(4):
        taps_of = blocks[block]

        def build(even_plane):
            def step(k, carry):
                rows = pl.ds(pl.multiple_of(k * 16, 16), 16)
                for side in range(2):
                    taps = []
                    for t in range(3):
                        merged = []
                        for j in range(3):
                            near, mid, far = (taps_of.at[9 * t + 3 * i + j] for i in range(3))
                            if side == 0:
                                g = near[rows, :] if even_plane else near[rows, :] + mid[rows, :]
                            else:
                                g = far[rows, :] + mid[rows, :] if even_plane else far[rows, :]
                            merged.append(g)
                        taps.append((merged[0] + merged[1] + merged[2], merged[0], merged[2]))
                    half = sides[1 + side]
                    dst = pl.ds(pl.multiple_of(half * 128 + k * 16, 16), 16)
                    slot = block if block in (0, 3) else (half if block == 2 else 1 - half) * -1 + 2
                    for v in range(3):
                        for m, value in enumerate(time_weights(taps[0][v], taps[1][v], taps[2][v])):
                            hi, lo = split(value)
                            done[slot, m, v, 0, dst, :] = hi
                            done[slot, m, v, 1, dst, :] = lo
                return carry

            lax.fori_loop(0, 8, step, 0)

        @pl.when(sides[0] == 0)
        def _():
            build(True)

        @pl.when(sides[0] == 1)
        def _():
            build(False)

        for k in ((0,), (), (1, 2), (3,))[block]:
            flush(k).start()
    for k in range(4):
        flush(k).wait()


W2S = (4, 4, 3, 2, 256, 256)


def run_prep(sides, blocks):
    return pl.pallas_call(
        prep_second,
        in_specs=[INS] + [INV] * 4,
        out_specs=INH,
        scratch_shapes=[pltpu.VMEM(W2S, BF16), pltpu.SemaphoreType.DMA((4,))],
        out_shape=pltpu.HBM(W2S, BF16),
        compiler_params=pltpu.CompilerParams(vmem_limit_bytes=15 * MB),
        cost_estimate=pl.CostEstimate(flops=1_000_000, bytes_accessed=4_000_000, transcendentals=0),
        name="prep_second",
    )(sides, *blocks)


def rows_of(even, odd):
    return lambda t: even[t], lambda t: odd[t]


def norm_silu(ids, slots, valid, pair, stats, h):
    count = float(T * 2 * Q * GW)
    terms = []
    for k in slots:
        block = ids[k]
        means = stats[:, block, 0, :]
        mean = means.sum(0, keepdims=True) / NR
        off = means - mean
        m2 = stats[:, block, 1, :].sum(0, keepdims=True) + count * (off * off).sum(0, keepdims=True)
        scale = stats[0, block, 2:3, :] / jnp.sqrt(m2 / (count * NR) + EPS)
        terms.append((mean, scale, stats[0, block, 3:4, :]))

    def norm(t, carry):
        for side, (mean, scale, shift) in enumerate(terms):
            v = (pair[side](t) - mean) * scale + shift
            v = v / (1.0 + jnp.exp(-v))
            h[t, :, side * 128 : side * 128 + 128] = v * valid[side]
        return carry

    lax.fori_loop(0, T, norm, 0)


def fill_a(h, a):
    def fill(side, carry):
        lanes = pl.ds(pl.multiple_of(side * 128, 128), 128)
        x = time_inputs(*(h[t, :, lanes] for t in range(T)))
        for f in range(6):
            for v, value in enumerate((x[f], shifted(x[f], 1) - x[f], shifted(x[f], -1) - x[f])):
                hi, lo = split(value)
                a[v, 0, f, :, lanes] = hi
                a[v, 1, f, :, lanes] = lo
        return carry

    lax.fori_loop(0, 2, fill, 0)


def multiply_second(a, w, before, acc):
    for v in range(3):
        for m, at, n in ((0, 0, 2), (1, 2, 2), (2, 4, 1), (3, 5, 1)):
            hi, lo = (a[v, k, at : at + n].reshape(n * Q, 256) for k in range(2))
            new = jnp.dot(
                jnp.concatenate([hi, hi, lo], axis=1),
                jnp.concatenate([w[m, v, 0], w[m, v, 1], w[m, v, 0]], axis=0),
                preferred_element_type=F32,
            ).reshape(n, Q, 256)
            acc[v, at : at + n] = new if before is None else before[v, at : at + n] + new


def conv2_early(ids, valid, e1, o3, stats, w, acc, w2, h, a, w1, sems):
    fetches = [pltpu.make_async_copy(w.at[k + 1], to, sems.at[k]) for k, to in enumerate((w1, w2))]
    for fetch in fetches:
        fetch.start()
    norm_silu(ids, (1, 2), valid, rows_of(e1, o3), stats, h)
    fill_a(h, a)
    fetches[0].wait()
    multiply_second(a, w1, None, acc)
    fetches[1].wait()


def conv2_late(ids, valid, e3, o1, stats, w, w2, before, acc, w0, w3, h, a, sems):
    fetches = [pltpu.make_async_copy(w.at[3 * k], to, sems.at[k]) for k, to in enumerate((w0, w3))]
    for fetch in fetches:
        fetch.start()
    norm_silu(ids, (2, 1), valid, rows_of(e3, o1), stats, h)
    fill_a(h, a)
    multiply_second(a, w2, before, acc)
    for fetch in fetches:
        fetch.wait()


def conv2_last(ids, valid, e0, o0, halo, e2, o2, stats, w0, w3, before, bias, out, h, a, acc, fine, sems):
    plane = ids[0]
    own = (
        lambda t: jnp.where(plane == 3, halo[t], e0[t]),
        lambda t: jnp.where(plane == 0, halo[t], o0[t]),
    )
    for slots, pair, w in (((0, 0), own, w0), ((3, 3), rows_of(e2, o2), w3)):
        norm_silu(ids, slots, valid, pair, stats, h)
        fill_a(h, a)
        multiply_second(a, w, before if w is w0 else acc, acc)
    copies = []
    for half in range(2):
        lanes = slice(half * 128, half * 128 + 128)
        y = time_outputs(*(acc[0, f, :, lanes] for f in range(6)))
        for v in (1, 2):
            z = time_outputs(*(acc[v, f, :, lanes] for f in range(6)))
            for t in range(T):
                fine[half, t, pl.ds(v - 1, Q, stride=2), :] = y[t] + z[t] + bias[:, lanes]
        copies.append(pltpu.make_async_copy(fine.at[half], out.at[:, :, lanes], sems.at[half]))
        copies[half].start()
    for copy in copies:
        copy.wait()


SUMS = (3, 6, Q, 256)
CONV2_SCRATCH = [pltpu.VMEM((T, Q, 256), F32), pltpu.VMEM((3, 2, 6, Q, 256), BF16)]


WEIGHTS = jax.ShapeDtypeStruct(W2S[1:], BF16)
ACC = jax.ShapeDtypeStruct(SUMS, F32)


def run_conv2_early(ids, valid, rows, stats, w):
    return pl.pallas_call(
        conv2_early,
        in_specs=[INS, INS] + [INV] * 3 + [INH],
        out_specs=[INV] * 2,
        scratch_shapes=CONV2_SCRATCH + [pltpu.VMEM(W2S[1:], BF16), pltpu.SemaphoreType.DMA((2,))],
        out_shape=[ACC, WEIGHTS],
        compiler_params=pltpu.CompilerParams(vmem_limit_bytes=10 * MB),
        cost_estimate=pl.CostEstimate(flops=2_300_000_000, bytes_accessed=7_000_000, transcendentals=200_000),
        name="conv2_early",
    )(ids, valid, *rows, stats, pltpu.with_memory_space_constraint(w, pltpu.HBM))


def run_conv2_late(ids, valid, rows, stats, w, w2, before):
    return pl.pallas_call(
        conv2_late,
        in_specs=[INS, INS] + [INV] * 3 + [INH] + [INV] * 2,
        out_specs=[INV] * 3,
        scratch_shapes=CONV2_SCRATCH + [pltpu.SemaphoreType.DMA((2,))],
        out_shape=[ACC, WEIGHTS, WEIGHTS],
        compiler_params=pltpu.CompilerParams(vmem_limit_bytes=8 * MB),
        cost_estimate=pl.CostEstimate(flops=2_300_000_000, bytes_accessed=7_000_000, transcendentals=200_000),
        name="conv2_late",
    )(ids, valid, *rows, stats, pltpu.with_memory_space_constraint(w, pltpu.HBM), w2, before)


def run_conv2_last(ids, valid, rows, stats, w0, w3, before, bias):
    return pl.pallas_call(
        conv2_last,
        in_specs=[INS, INS] + [INV] * 10,
        out_specs=INH,
        scratch_shapes=CONV2_SCRATCH
        + [pltpu.VMEM(SUMS, F32), pltpu.VMEM((2, T, 2 * Q, 128), F32), pltpu.SemaphoreType.DMA((2,))],
        out_shape=pltpu.HBM((T, 2 * Q, 256), F32),
        compiler_params=pltpu.CompilerParams(vmem_limit_bytes=14 * MB),
        cost_estimate=pl.CostEstimate(flops=4_600_000_000, bytes_accessed=1_000_000, transcendentals=400_000),
        name="conv2_last",
    )(ids, valid, *rows, stats, w0, w3, before, bias)


def index(r, c):
    return r * NC + c


def holder(r, q, odd):
    if odd and q == 0:
        r += 1
    if not odd and q == 3:
        r -= 1
    return index(r % NR, q)


def row_perm(step, odd, hops):
    pairs = []
    for r in range(NR):
        for p in range(NC):
            a, b = (p + step * (hops - 1)) % NC, (p + step * hops) % NC
            source = index(r, p) if hops == 1 else holder(r, a, odd)
            pairs.append((source, holder(r, b, odd)))
    return pairs


def block(latent, first_weight, norm_gain, norm_shift, second_weight, out_bias):
    c = lax.axis_index("ch")
    r = lax.axis_index("rows")
    both = ("rows", "ch")
    here, head, tail = run_intake(latent)
    top = lax.ppermute(tail, "rows", [(i, i + 1) for i in range(NR - 1)])
    bot = lax.ppermute(head, "rows", [(i + 1, i) for i in range(NR - 1)])

    def ids(*shifts):
        return jnp.stack([(c + s) % NC for s in shifts]).astype(jnp.int32)

    up = [(i, (i + 1) % NC) for i in range(NC)]
    down = [((i + 1) % NC, i) for i in range(NC)]

    def send(v, perm):
        return lax.ppermute(v, "ch", perm)

    x, part, b, w1, w3, w0 = run_conv1_local(ids(2, 1, 3, 0), here, first_weight)
    far_lo, far_hi, x = run_conv1_edge(top, bot, x, part, b)
    got_lo, got_hi = send(far_lo, up), send(far_hi, down)
    order = ids(0, 3, 1, 2)
    up_lo, up_hi, down_lo, down_hi, *blocks = run_conv1_near(order, x, w1, w3, second_weight)
    b1, a1 = send(up_hi, up), send(down_lo, down)
    sum_lo, sum_hi = up_lo + got_lo, down_hi + got_hi
    a2, b2 = send(sum_lo, up), send(sum_hi, down)
    own_lo, own_hi = run_conv1_more(x, w0)

    near = jnp.where((c == 0) | (c == 3), 1, 0)
    sides = jnp.stack([c % 2, near, 1 - near]).astype(jnp.int32)
    tied = lax.optimization_barrier((*blocks, sum_hi))
    w2 = run_prep(sides, tied[:4])
    own_lo, w2 = lax.optimization_barrier((own_lo, w2))
    even, odd, edge_row, stats = run_finish(
        c[None].astype(jnp.int32), own_lo, own_hi, a1, a2, b1, b2, norm_gain[None], norm_shift[None]
    )

    def move(v, step, is_odd, hops):
        return lax.ppermute(v, both, row_perm(step, is_odd, hops))

    e1, o3 = move(even, 1, False, 1), move(odd, -1, True, 1)
    o1, e3 = move(odd, 1, True, 1), move(even, -1, False, 1)
    edge = [(index(i, 0), index(i + 1, 0)) for i in range(NR - 1)]
    edge += [(index(i + 1, 3), index(i, 3)) for i in range(NR - 1)]
    stats = lax.all_to_all(stats, both, 0, 0, tiled=True).reshape(NR, NC, 4, CB)
    e2, o2 = move(e1, 1, False, 2), move(o3, -1, True, 2)
    halo = lax.ppermute(edge_row, both, edge)

    valid = jnp.stack(
        [
            jnp.where((c == 3) & (r == NR - 1), 0.0, 1.0),
            jnp.where((c == 0) & (r == 0), 0.0, 1.0),
        ]
    ).astype(F32)
    sums, w2_late = run_conv2_early(order, valid, (e1, o3), stats, w2)
    sums, w2_own, w2_far = run_conv2_late(order, valid, (e3, o1), stats, w2, w2_late, sums)
    rows = (even, odd, halo, e2, o2)
    out = run_conv2_last(order, valid, rows, stats, w2_own, w2_far, sums, out_bias[None])
    return out[:, None]


def solution(mesh):
    return jax.shard_map(
        block,
        mesh=mesh,
        in_specs=(P(None, "rows", None, "ch"), P(None, "ch", None), P("ch"), P("ch"), P(), P()),
        out_specs=P(None, ("rows", "ch"), None, None),
        check_vma=False,
    )
```
